32 devices in a mesh: groups: 2 (over x), frame: 16 (over z, y, core).
Axes of the slice: x: 2, y: 2, z: 4, core: 2. Of those that a mesh axis runs over, the one named last changes fastest.
Arguments:
- lowres: bfloat16 [32, 64, 128], P(('groups', 'frame')), parts along dimension 0, may hold values from -6 to 6
- noisy: bfloat16 [32, 8, 64, 128], P(('groups', 'frame')), parts along dimension 0, may hold values from -6 to 6
- starts: int32 [8], P('groups'), parts along dimension 0, may hold values from 0 to 8, as said below
- blend: int32 [8, 8], P('groups'), parts along dimension 0, may hold values from 1 to 4
- assign: int32 [32], P('groups'), parts along dimension 0, may hold values from 0 to 15, each once
- base_w: bfloat16 [3, 128, 128], replicated, may hold values from -0.3125 to 0.3125
- cond_w: bfloat16 [128, 128], replicated, may hold values from -0.5 to 0.5
- noise_w: bfloat16 [128, 128], replicated, may hold values from -0.5 to 0.5
- gains: float32 [3, 128], replicated, may hold values from 0.25 to 1.75
- tconv: float32 [3, 3, 128], replicated, may hold values from -3 to 3
- mlp_in: bfloat16 [3, 128, 512], replicated, may hold values from -0.5 to 0.5
- mlp_out: bfloat16 [3, 512, 128], replicated, may hold values from -0.25 to 0.25
Outputs:
- video: bfloat16 [32, 256, 128], P(('groups', 'frame')), parts along dimension 0
The draws below stay inside these ranges and needn't reach their ends.
There are 2 independent parts, one for each index of `groups`. The reference program is written for one: setup_inputs(seed, part) draws one part's arguments, and reference() takes and returns one part's arrays. A program takes and returns all parts, laid end to end along the dimension named above; an argument that names none is the same for every part. Nothing has to cross between parts.
Inputs may be any that keep to these rules, and one draw needn't show every extreme that they name: Window k covers frames starts[k] to starts[k] + 7; every frame lies in some window; the first window starts at 0 and the last at 8.
All inputs are finite; a program needn't handle non-finite values.
Results may differ from the reference program's by a relative error of at most 0.0059.
Values may be sent and summed in bfloat16 or wider, within the bound.
No kernel may reach another device: no remote copies, remote signals or barrier semaphores. Data moves between devices by JAX's collectives and lax.ppermute only.
A program may use at most 64 MiB of HBM per device.

```python
import jax
import jax.numpy as jnp
from jax import lax

C = 128
HID = 512
L = 8
TILES = 4
LAYERS = 3
TP = 64
PL = 16
FRAMES = 16
NWIN = 4


def draw_starts(key, part):
    window_ids = jnp.arange(NWIN, dtype=jnp.int32)
    spaced = window_ids * (FRAMES - L) // (NWIN - 1)
    jitter = jax.random.randint(jax.random.fold_in(key, 17), (NWIN,), -2, 3)
    placed = jnp.clip(spaced + jitter, 0, FRAMES - L)
    placed = jnp.where(window_ids == 0, 0, placed)
    placed = jnp.where(window_ids == NWIN - 1, FRAMES - L, placed)
    return placed.astype(jnp.int32)


def place_ends(values, key, smallest, top_value):
    spot = [jax.random.randint(jax.random.fold_in(key, axis), (), 0, length) for axis, length in enumerate(values.shape)]
    longest = values.shape.index(max(values.shape))
    neighbour = spot[:longest] + [(spot[longest] + 1) % values.shape[longest]] + spot[longest + 1:]
    return values.at[tuple(spot)].set(smallest).at[tuple(neighbour)].set(top_value)


def block_levels(key, extent, split, smallest, top_value):
    def one(axis_at, parts):
        steps = jax.random.uniform(jax.random.fold_in(jax.random.fold_in(key, 6), axis_at), (parts,), jnp.float32, smallest / len(split), top_value / len(split))
        return jnp.repeat(jnp.exp(steps), extent[axis_at] // parts).reshape((-1,) + (1,) * (len(extent) - axis_at - 1))

    level = one(*split[0])
    for cut in split[1:]:
        level = level * one(*cut)
    return level


def noise(own_key, shape, spread, reach, split=(), held_as=jnp.bfloat16):
    level = block_levels(own_key, shape, split, -0.22, 0.18) if split else 1.0
    array = jax.random.normal(own_key, shape, jnp.float32) * spread * level
    return jnp.minimum(jnp.maximum(array, -reach), reach).astype(held_as)


def setup_inputs(seed: int = 0, part: int = 0) -> dict:
    key_list = jax.random.split(jax.random.key(seed), 13)
    part_splits = jax.random.split(jax.random.fold_in(key_list[12], part), 13)
    return {
        "lowres": noise(part_splits[0], (FRAMES, TILES * PL, C), 1.0, 6.0, ((0, 16),)),
        "noisy": noise(part_splits[1], (FRAMES, L, TP, C), 1.0, 6.0, ((0, 16),)),
        "starts": draw_starts(jax.random.fold_in(jax.random.fold_in(key_list[12], part), 71), part),
        "blend": place_ends(jax.random.randint(part_splits[3], (NWIN, L), 1, 5), jax.random.fold_in(part_splits[3], 1), 1, 4).astype(jnp.int32),
        "assign": jax.random.permutation(part_splits[4], FRAMES).astype(jnp.int32),
        "base_w": noise(key_list[5], (3, C, C), (3 * C) ** -0.5, 0.3125),
        "cond_w": noise(key_list[6], (C, C), C ** -0.5, 0.5),
        "noise_w": noise(key_list[7], (C, C), C ** -0.5, 0.5),
        "gains": jnp.clip(1.0 + 0.15 * jax.random.normal(key_list[8], (LAYERS, C), jnp.float32), 0.25, 1.75),
        "tconv": noise(key_list[9], (LAYERS, 3, C), 0.5, 3.0, (), jnp.float32),
        "mlp_in": noise(key_list[10], (LAYERS, C, HID), C ** -0.5, 0.5),
        "mlp_out": noise(key_list[11], (LAYERS, HID, C), HID ** -0.5, 0.25),
    }


def base_frames(lowres, base_w):
    zeros_frame = jnp.zeros_like(lowres[:1])
    before = jnp.concatenate([zeros_frame, lowres[:-1]], 0)
    behind = jnp.concatenate([lowres[1:], zeros_frame], 0)
    row_count = lowres.shape[0] * lowres.shape[1]
    channels = lowres.shape[2]
    total = jnp.dot(before.reshape(row_count, channels), base_w[0], preferred_element_type=jnp.float32)
    total = total + jnp.dot(lowres.reshape(row_count, channels), base_w[1], preferred_element_type=jnp.float32)
    total = total + jnp.dot(behind.reshape(row_count, channels), base_w[2], preferred_element_type=jnp.float32)
    result = lowres.astype(jnp.float32) + jax.nn.silu(total).reshape(lowres.shape)
    return result.astype(jnp.bfloat16)

def refine(cond, noisy_item, cond_w, noise_w, gains, tconv, mlp_in, mlp_out):
    frame_count, positions, channels = cond.shape
    row_count = frame_count * positions
    state = jnp.dot(cond.reshape(row_count, channels), cond_w, preferred_element_type=jnp.float32)
    state = state + jnp.dot(noisy_item.reshape(row_count, channels), noise_w, preferred_element_type=jnp.float32)
    for layer_id in range(gains.shape[0]):
        inverse = lax.rsqrt(lax.optimization_barrier(jnp.mean(state * state, axis=-1, keepdims=True)) + 1e-06)
        normed = (state * inverse * gains[layer_id]).reshape(frame_count, positions, channels)
        zeros_frame = jnp.zeros_like(normed[:1])
        before = jnp.concatenate([zeros_frame, normed[:-1]], 0)
        behind = jnp.concatenate([normed[1:], zeros_frame], 0)
        mixed_rows = normed + tconv[layer_id, 0] * before + tconv[layer_id, 1] * normed + tconv[layer_id, 2] * behind
        mixed_rows = mixed_rows.reshape(row_count, channels).astype(jnp.bfloat16)
        hidden = jax.nn.silu(jnp.dot(mixed_rows, mlp_in[layer_id], preferred_element_type=jnp.float32)).astype(jnp.bfloat16)
        state = state + jnp.dot(hidden, mlp_out[layer_id], preferred_element_type=jnp.float32)
    return state.astype(jnp.bfloat16).reshape(frame_count, positions, channels)

def reference(lowres, noisy, starts, blend, assign, base_w, cond_w, noise_w, gains, tconv, mlp_in, mlp_out):
    base_all = base_frames(lowres, base_w)
    tiled = base_all.reshape(FRAMES, TILES, PL, C)
    zero_index = jnp.zeros((), jnp.int32)

    def one_slot(totals, slot_id):
        item_id = assign[slot_id].astype(jnp.int32)
        window_id = (item_id // TILES).astype(jnp.int32)
        tile_id = (item_id % TILES).astype(jnp.int32)
        first = starts[window_id].astype(jnp.int32)
        window_tiles = lax.dynamic_slice(tiled, (first, tile_id, zero_index, zero_index), (L, 1, PL, C))[:, 0]
        cond = jnp.repeat(window_tiles, 4, axis=1)
        refined = refine(cond, noisy[slot_id], cond_w, noise_w, gains, tconv, mlp_in, mlp_out)
        factor = blend[window_id].astype(jnp.float32)
        current = lax.dynamic_slice(totals, (first, tile_id, zero_index, zero_index), (L, 1, TP, C))
        updated = current + (factor[:, None, None] * refined.astype(jnp.float32))[:, None]
        totals = lax.dynamic_update_slice(totals, updated, (first, tile_id, zero_index, zero_index))
        return (totals, None)
    totals = jnp.zeros((FRAMES, TILES, TP, C), jnp.float32)
    totals, _ = lax.scan(one_slot, totals, jnp.arange(FRAMES, dtype=jnp.int32))
    covered = (starts[:, None] + jnp.arange(L, dtype=jnp.int32)[None, :]).astype(jnp.int32)
    denom = jax.ops.segment_sum(blend.reshape(-1).astype(jnp.float32), covered.reshape(-1), FRAMES)
    video = totals / denom[:, None, None, None]
    return video.reshape(FRAMES, TILES * TP, C).astype(jnp.bfloat16)
```

```python
import functools

import jax
import jax.numpy as jnp
from jax import lax
from jax.experimental import pallas as pl
from jax.experimental.pallas import tpu as pltpu
from jax.sharding import PartitionSpec as P

F32 = jnp.float32
BF16 = jnp.bfloat16
VMEM = pltpu.VMEM
SMEM = pltpu.SMEM


def dot(a, b):
    return jnp.dot(a, b, preferred_element_type=F32)


def silu(x):
    half = 0.5 * x
    return half + half * jnp.tanh(half)


def spec(space):
    return pl.BlockSpec(memory_space=space)


def pick_kernel(tiles, assign_ref, low_ref, out_ref):
    count, low_pos, _ = out_ref.shape

    def body(slot, carry):
        tile = lax.rem(assign_ref[slot], tiles)
        first = pl.multiple_of(tile * low_pos, low_pos)
        out_ref[slot] = low_ref[0, pl.ds(first, low_pos), :]
        return carry

    lax.fori_loop(0, count, body, 0, unroll=min(count, 16))


def side_kernel(
    tiles, assign_ref, starts_ref, blend_ref, noisy_ref, noise_w_ref,
    projected_ref, picker_ref, weights_ref, placed_ref,
):
    count = assign_ref.shape[0]
    windows, window_len = blend_ref.shape
    channels = noisy_ref.shape[-1]
    tile_pos = noisy_ref.shape[2]
    rows, low_rows = picker_ref.shape
    low_pos = low_rows // count
    own = lax.axis_index("frame")
    projected_ref[...] = dot(noisy_ref[0].reshape(rows, channels), noise_w_ref[...])
    start = starts_ref[assign_ref[own] // tiles]
    row = lax.broadcasted_iota(jnp.int32, (rows, low_rows), 0)
    column = lax.broadcasted_iota(jnp.int32, (rows, low_rows), 1)
    wanted = row // (tile_pos // low_pos) + start * low_pos
    picker_ref[...] = jnp.where(column == wanted, 1.0, 0.0).astype(BF16)
    placed_ref[...] = jnp.zeros_like(placed_ref)

    def factor_of(window):
        offset = own - starts_ref[window]
        inside = (offset >= 0) & (offset < window_len)
        clipped = jnp.clip(offset, 0, window_len - 1)
        return jnp.where(inside, blend_ref[window, clipped], 0)

    denom = lax.fori_loop(
        0, windows, lambda w, total: total + factor_of(w), jnp.int32(0), unroll=min(windows, 4)
    )
    denom_row = jnp.full((1, channels), denom, jnp.int32).astype(F32)
    weights_ref[...] = jnp.zeros_like(weights_ref)

    def body(slot, carry):
        item = assign_ref[slot]
        factor = factor_of(item // tiles)
        factor_row = jnp.full((1, channels), factor, jnp.int32).astype(F32)
        weights_ref[slot, pl.ds(lax.rem(item, tiles), 1), :] = factor_row / denom_row
        return carry

    lax.fori_loop(0, count, body, 0)


def refine_kernel(
    tiles, assign_hbm, starts_hbm, tile_ref, projected_ref, picker_ref, base_w_ref, cond_w_ref,
    gains_ref, tconv_ref, mlp_in_ref, mlp_out_ref, zeros_hbm, placed_hbm,
    assign_sm, starts_sm, refined_ref, sems,
):
    copies = [
        pltpu.make_async_copy(assign_hbm, assign_sm, sems.at[0]),
        pltpu.make_async_copy(starts_hbm, starts_sm, sems.at[1]),
    ]
    for copy in copies:
        copy.start()
    count, low_pos, channels = tile_ref.shape
    window_len, tile_pos, _ = refined_ref.shape
    rows = window_len * tile_pos
    frames = tile_ref[...]
    edge = jnp.zeros((1, low_pos, channels), BF16)
    before = jnp.concatenate([edge, frames[:-1]], 0).reshape(count * low_pos, channels)
    behind = jnp.concatenate([frames[1:], edge], 0).reshape(count * low_pos, channels)
    middle = frames.reshape(count * low_pos, channels)
    total = dot(before, base_w_ref[0]) + dot(middle, base_w_ref[1]) + dot(behind, base_w_ref[2])
    base = (middle.astype(F32) + silu(total)).astype(BF16)
    cond = dot(picker_ref[...], base).astype(BF16)
    state = dot(cond, cond_w_ref[...]) + projected_ref[...]
    layers = gains_ref.shape[0]
    for layer in range(layers):
        inverse = lax.rsqrt(jnp.mean(state * state, axis=-1, keepdims=True) + 1e-06)
        normed = (state * inverse * gains_ref[layer : layer + 1, :]).reshape(
            window_len, tile_pos, channels
        )
        edge = jnp.zeros((1, tile_pos, channels), F32)
        before = jnp.concatenate([edge, normed[:-1]], 0)
        behind = jnp.concatenate([normed[1:], edge], 0)
        mixed = (
            normed
            + tconv_ref[layer, 0:1, :] * before
            + tconv_ref[layer, 1:2, :] * normed
            + tconv_ref[layer, 2:3, :] * behind
        )
        mixed = mixed.reshape(rows, channels).astype(BF16)
        pieces = []
        step = rows // CHUNKS
        for piece in range(CHUNKS):
            part = slice(piece * step, (piece + 1) * step)
            hidden = silu(dot(mixed[part], mlp_in_ref[layer])).astype(BF16)
            pieces.append(state[part] + dot(hidden, mlp_out_ref[layer]))
        state = jnp.concatenate(pieces, 0) if len(pieces) > 1 else pieces[0]
    refined_ref[...] = state.astype(BF16).reshape(window_len, tile_pos, channels)
    for copy in copies:
        copy.wait()
    start = starts_sm[assign_sm[lax.axis_index("frame")] // tiles]
    out = pltpu.make_async_copy(refined_ref, placed_hbm.at[pl.ds(start, window_len)], sems.at[2])
    out.start()
    out.wait()


CHUNKS = 4


def blend_kernel(received_ref, weights_ref, video_ref):
    count, tile_pos, channels = received_ref.shape
    tiles = weights_ref.shape[1]

    def body(slot, totals):
        rows = received_ref[slot].astype(F32)
        weights = weights_ref[slot]
        return tuple(totals[t] + weights[t : t + 1, :] * rows for t in range(tiles))

    zero = jnp.zeros((tile_pos, channels), F32)
    totals = lax.fori_loop(0, count, body, (zero,) * tiles, unroll=min(count, 16))
    for t in range(tiles):
        video_ref[0, t * tile_pos : (t + 1) * tile_pos, :] = totals[t].astype(BF16)


def on_device(
    lowres, noisy, starts, blend, assign, base_w, cond_w, noise_w, gains, tconv, mlp_in, mlp_out
):
    count = assign.shape[0]
    windows, window_len = blend.shape
    tiles = count // windows
    tile_pos, channels = noisy.shape[2:]
    low_pos = lowres.shape[1] // tiles
    rows = window_len * tile_pos
    hidden = mlp_in.shape[-1]
    layers = gains.shape[0]

    outgoing = pl.pallas_call(
        functools.partial(pick_kernel, tiles),
        out_shape=jax.ShapeDtypeStruct((count, low_pos, channels), BF16),
        in_specs=[spec(SMEM), spec(VMEM)],
        out_specs=spec(VMEM),
        name="pick",
    )(assign, lowres)
    gathered = lax.all_to_all(outgoing, "frame", split_axis=0, concat_axis=0, tiled=True)

    projected, picker, weights, zeros = pl.pallas_call(
        functools.partial(side_kernel, tiles),
        out_shape=(
            jax.ShapeDtypeStruct((rows, channels), F32),
            jax.ShapeDtypeStruct((rows, count * low_pos), BF16),
            jax.ShapeDtypeStruct((count, tiles, channels), F32),
            jax.ShapeDtypeStruct((count, tile_pos, channels), BF16),
        ),
        in_specs=[spec(SMEM)] * 3 + [spec(VMEM)] * 2,
        out_specs=(spec(VMEM),) * 4,
        cost_estimate=pl.CostEstimate(
            flops=2 * rows * channels * channels, bytes_accessed=4 * rows * channels, transcendentals=0
        ),
        name="side",
    )(assign, starts, blend, noisy, noise_w)

    placed = pl.pallas_call(
        functools.partial(refine_kernel, tiles),
        out_shape=jax.ShapeDtypeStruct((count, tile_pos, channels), BF16),
        in_specs=[spec(pl.ANY)] * 2 + [spec(VMEM)] * 9 + [spec(pl.ANY)],
        out_specs=spec(pl.ANY),
        scratch_shapes=[
            SMEM(assign.shape, jnp.int32),
            SMEM(starts.shape, jnp.int32),
            VMEM((window_len, tile_pos, channels), BF16),
            pltpu.SemaphoreType.DMA((3,)),
        ],
        input_output_aliases={11: 0},
        cost_estimate=pl.CostEstimate(
            flops=4 * layers * rows * channels * hidden,
            bytes_accessed=4 * layers * channels * hidden,
            transcendentals=layers * rows * hidden,
        ),
        name="refine",
    )(
        assign, starts, gathered, projected, picker, base_w, cond_w, gains, tconv, mlp_in, mlp_out,
        zeros,
    )
    received = lax.all_to_all(placed, "frame", split_axis=0, concat_axis=0, tiled=True)
    return pl.pallas_call(
        blend_kernel,
        out_shape=jax.ShapeDtypeStruct((1, tiles * tile_pos, channels), BF16),
        in_specs=[spec(VMEM)] * 2,
        out_specs=spec(VMEM),
        name="blend",
    )(received, weights)


def solution(mesh):
    in_specs = (
        P(("groups", "frame"), None, None),
        P(("groups", "frame"), None, None, None),
        P("groups"),
        P("groups", None),
        P("groups"),
        P(),
        P(),
        P(),
        P(),
        P(),
        P(),
        P(),
    )
    out_specs = P(("groups", "frame"), None, None)
    return jax.shard_map(
        on_device, mesh=mesh, in_specs=in_specs, out_specs=out_specs, check_vma=False
    )
```

```python
import functools

import jax
import jax.numpy as jnp
from jax import lax
from jax.experimental import pallas as pl
from jax.experimental.pallas import tpu as pltpu
from jax.sharding import PartitionSpec as P

F32 = jnp.float32
BF16 = jnp.bfloat16
VMEM = pltpu.VMEM
SMEM = pltpu.SMEM
ROOM = 24 << 20


def dot(a, b):
    return jnp.dot(a, b, preferred_element_type=F32)


def silu(x):
    half = 0.5 * x
    return half + half * jnp.tanh(half)


def spec(space):
    return pl.BlockSpec(memory_space=space)


def near(*arrays):
    return tuple(pltpu.with_memory_space_constraint(array, VMEM) for array in arrays)


def far(*arrays):
    return tuple(pltpu.with_memory_space_constraint(array, pltpu.HBM) for array in arrays)


def pick_kernel(tiles, assign_ref, low_ref, out_ref):
    count, low_pos, _ = out_ref.shape

    def body(slot, carry):
        tile = lax.rem(assign_ref[slot], tiles)
        first = pl.multiple_of(tile * low_pos, low_pos)
        out_ref[slot] = low_ref[0, pl.ds(first, low_pos), :]
        return carry

    lax.fori_loop(0, count, body, 0, unroll=min(count, 16))


def side_kernel(
    tiles, assign_ref, starts_ref, blend_ref, noisy_ref, noise_w_ref, *refs
):
    moved = (len(refs) - 5) // 2
    sources, targets, sems = refs[:moved], refs[moved + 4 : -1], refs[-1]
    projected_ref, picker_ref, weights_ref, placed_ref = refs[moved : moved + 4]
    copies = [
        pltpu.make_async_copy(source, target, sems.at[k])
        for k, (source, target) in enumerate(zip(sources, targets))
    ]
    for copy in copies:
        copy.start()
    count = assign_ref.shape[0]
    windows, window_len = blend_ref.shape
    channels = noisy_ref.shape[-1]
    tile_pos = noisy_ref.shape[2]
    rows, low_rows = picker_ref.shape
    low_pos = low_rows // count
    own = lax.axis_index("frame")
    projected_ref[...] = dot(noisy_ref[0].reshape(rows, channels), noise_w_ref[...])
    start = starts_ref[assign_ref[own] // tiles]
    row = lax.broadcasted_iota(jnp.int32, (rows, low_rows), 0)
    column = lax.broadcasted_iota(jnp.int32, (rows, low_rows), 1)
    wanted = row // (tile_pos // low_pos) + start * low_pos
    picker_ref[...] = jnp.where(column == wanted, 1.0, 0.0).astype(BF16)
    placed_ref[...] = jnp.zeros_like(placed_ref)

    def factor_of(window):
        offset = own - starts_ref[window]
        inside = (offset >= 0) & (offset < window_len)
        clipped = jnp.clip(offset, 0, window_len - 1)
        return jnp.where(inside, blend_ref[window, clipped], 0)

    denom = lax.fori_loop(
        0, windows, lambda w, total: total + factor_of(w), jnp.int32(0), unroll=min(windows, 4)
    )
    denom_row = jnp.full((1, channels), denom, jnp.int32).astype(F32)
    weights_ref[...] = jnp.zeros_like(weights_ref)

    def body(slot, carry):
        item = assign_ref[slot]
        factor = factor_of(item // tiles)
        factor_row = jnp.full((1, channels), factor, jnp.int32).astype(F32)
        weights_ref[slot, pl.ds(lax.rem(item, tiles), 1), :] = factor_row / denom_row
        return carry

    lax.fori_loop(0, count, body, 0)
    for copy in copies:
        copy.wait()


def refine_kernel(
    tiles, assign_hbm, starts_hbm, tile_ref, projected_ref, picker_ref, base_w_ref, cond_w_ref,
    gains_ref, tconv_ref, mlp_in_ref, mlp_out_ref, zeros_ref, placed_ref,
    assign_sm, starts_sm, sems,
):
    copies = [
        pltpu.make_async_copy(assign_hbm, assign_sm, sems.at[0]),
        pltpu.make_async_copy(starts_hbm, starts_sm, sems.at[1]),
    ]
    for copy in copies:
        copy.start()
    count, low_pos, channels = tile_ref.shape
    rows = projected_ref.shape[0]
    tile_pos = placed_ref.shape[1]
    window_len = rows // tile_pos
    frames = tile_ref[...]
    edge = jnp.zeros((1, low_pos, channels), BF16)
    before = jnp.concatenate([edge, frames[:-1]], 0).reshape(count * low_pos, channels)
    behind = jnp.concatenate([frames[1:], edge], 0).reshape(count * low_pos, channels)
    middle = frames.reshape(count * low_pos, channels)
    total = dot(before, base_w_ref[0]) + dot(middle, base_w_ref[1]) + dot(behind, base_w_ref[2])
    base = (middle.astype(F32) + silu(total)).astype(BF16)
    cond = dot(picker_ref[...], base).astype(BF16)
    state = dot(cond, cond_w_ref[...]) + projected_ref[...]
    layers = gains_ref.shape[0]
    for layer in range(layers):
        inverse = lax.rsqrt(jnp.mean(state * state, axis=-1, keepdims=True) + 1e-06)
        normed = (state * inverse * gains_ref[layer : layer + 1, :]).reshape(
            window_len, tile_pos, channels
        )
        edge = jnp.zeros((1, tile_pos, channels), F32)
        before = jnp.concatenate([edge, normed[:-1]], 0)
        behind = jnp.concatenate([normed[1:], edge], 0)
        mixed = (
            normed
            + tconv_ref[layer, 0:1, :] * before
            + tconv_ref[layer, 1:2, :] * normed
            + tconv_ref[layer, 2:3, :] * behind
        )
        mixed = mixed.reshape(rows, channels).astype(BF16)
        pieces = []
        step = rows // CHUNKS
        for piece in range(CHUNKS):
            part = slice(piece * step, (piece + 1) * step)
            hidden = silu(dot(mixed[part], mlp_in_ref[layer])).astype(BF16)
            pieces.append(state[part] + dot(hidden, mlp_out_ref[layer]))
        state = jnp.concatenate(pieces, 0) if len(pieces) > 1 else pieces[0]
    for copy in copies:
        copy.wait()
    start = starts_sm[assign_sm[lax.axis_index("frame")] // tiles]
    placed_ref[pl.ds(start, window_len)] = state.astype(BF16).reshape(
        window_len, tile_pos, channels
    )


CHUNKS = 4


def blend_kernel(received_ref, weights_ref, video_ref):
    count, tile_pos, channels = received_ref.shape
    tiles = weights_ref.shape[1]

    def body(slot, totals):
        rows = received_ref[slot].astype(F32)
        weights = weights_ref[slot]
        return tuple(totals[t] + weights[t : t + 1, :] * rows for t in range(tiles))

    zero = jnp.zeros((tile_pos, channels), F32)
    totals = lax.fori_loop(0, count, body, (zero,) * tiles, unroll=min(count, 16))
    for t in range(tiles):
        video_ref[0, t * tile_pos : (t + 1) * tile_pos, :] = totals[t].astype(BF16)


def on_device(
    lowres, noisy, starts, blend, assign, base_w, cond_w, noise_w, gains, tconv, mlp_in, mlp_out
):
    count = assign.shape[0]
    windows, window_len = blend.shape
    tiles = count // windows
    tile_pos, channels = noisy.shape[2:]
    low_pos = lowres.shape[1] // tiles
    rows = window_len * tile_pos
    hidden = mlp_in.shape[-1]
    layers = gains.shape[0]

    outgoing = pl.pallas_call(
        functools.partial(pick_kernel, tiles),
        out_shape=VMEM((count, low_pos, channels), BF16),
        in_specs=[spec(SMEM), spec(VMEM)],
        out_specs=spec(VMEM),
        compiler_params=pltpu.CompilerParams(vmem_limit_bytes=ROOM),
        name="pick",
    )(*far(assign, lowres))
    gathered = lax.all_to_all(outgoing, "frame", split_axis=0, concat_axis=0, tiled=True)

    moved = (base_w, cond_w, gains, tconv, mlp_in, mlp_out)
    projected, picker, weights, zeros, *params = pl.pallas_call(
        functools.partial(side_kernel, tiles),
        out_shape=(
            VMEM((rows, channels), F32),
            VMEM((rows, count * low_pos), BF16),
            VMEM((count, tiles, channels), F32),
            VMEM((count, tile_pos, channels), BF16),
            *(VMEM(array.shape, array.dtype) for array in moved),
        ),
        in_specs=[spec(SMEM)] * 3 + [spec(VMEM)] * 2 + [spec(pl.ANY)] * len(moved),
        out_specs=(spec(VMEM),) * (4 + len(moved)),
        scratch_shapes=[pltpu.SemaphoreType.DMA((len(moved),))],
        cost_estimate=pl.CostEstimate(
            flops=2 * rows * channels * channels, bytes_accessed=4 * rows * channels, transcendentals=0
        ),
        compiler_params=pltpu.CompilerParams(vmem_limit_bytes=ROOM),
        name="side",
    )(*far(assign, starts, blend, noisy, noise_w, *moved))

    placed = pl.pallas_call(
        functools.partial(refine_kernel, tiles),
        out_shape=VMEM((count, tile_pos, channels), BF16),
        in_specs=[spec(pl.ANY)] * 2 + [spec(VMEM)] * 10,
        out_specs=spec(VMEM),
        scratch_shapes=[
            SMEM(assign.shape, jnp.int32),
            SMEM(starts.shape, jnp.int32),
            pltpu.SemaphoreType.DMA((2,)),
        ],
        input_output_aliases={11: 0},
        cost_estimate=pl.CostEstimate(
            flops=4 * layers * rows * channels * hidden,
            bytes_accessed=4 * layers * channels * hidden,
            transcendentals=layers * rows * hidden,
        ),
        compiler_params=pltpu.CompilerParams(vmem_limit_bytes=ROOM),
        name="refine",
    )(
        *far(assign, starts),
        *near(gathered, projected, picker, *params, zeros),
    )
    received = lax.all_to_all(placed, "frame", split_axis=0, concat_axis=0, tiled=True)
    return pl.pallas_call(
        blend_kernel,
        out_shape=jax.ShapeDtypeStruct((1, tiles * tile_pos, channels), BF16),
        in_specs=[spec(VMEM)] * 2,
        out_specs=spec(VMEM),
        compiler_params=pltpu.CompilerParams(vmem_limit_bytes=ROOM),
        name="blend",
    )(*near(received, weights))


def solution(mesh):
    in_specs = (
        P(("groups", "frame"), None, None),
        P(("groups", "frame"), None, None, None),
        P("groups"),
        P("groups", None),
        P("groups"),
        P(),
        P(),
        P(),
        P(),
        P(),
        P(),
        P(),
    )
    out_specs = P(("groups", "frame"), None, None)
    return jax.shard_map(
        on_device, mesh=mesh, in_specs=in_specs, out_specs=out_specs, check_vma=False
    )
```

```python
import functools

import jax
import jax.numpy as jnp
from jax import lax
from jax.experimental import pallas as pl
from jax.experimental.pallas import tpu as pltpu
from jax.sharding import PartitionSpec as P

F32 = jnp.float32
BF16 = jnp.bfloat16
VMEM = pltpu.VMEM
SMEM = pltpu.SMEM
ROOM = 24 << 20


def dot(a, b):
    return jnp.dot(a, b, preferred_element_type=F32)


def silu(x):
    half = 0.5 * x
    return half + half * jnp.tanh(half)


def spec(space):
    return pl.BlockSpec(memory_space=space)


def near(*arrays):
    return tuple(pltpu.with_memory_space_constraint(array, VMEM) for array in arrays)


def far(*arrays):
    return tuple(pltpu.with_memory_space_constraint(array, pltpu.HBM) for array in arrays)


def rank_of(frame, count):
    return lax.rem(frame + count // 2, jnp.int32(count))


def exchange(blocks):
    count = blocks.shape[0]
    order = [(rank + count // 2) % count for rank in range(count)]
    return lax.all_to_all(
        blocks, "frame", split_axis=0, concat_axis=0, tiled=True, axis_index_groups=[order]
    )


def pick_kernel(tiles, assign_ref, low_ref, out_ref):
    count, low_pos, _ = out_ref.shape

    def body(slot, carry):
        tile = lax.rem(assign_ref[slot], tiles)
        first = pl.multiple_of(tile * low_pos, low_pos)
        out_ref[rank_of(slot, count)] = low_ref[0, pl.ds(first, low_pos), :]
        return carry

    lax.fori_loop(0, count, body, 0, unroll=min(count, 16))


def side_kernel(
    tiles, assign_ref, starts_ref, blend_ref, noisy_ref, noise_w_ref, *refs
):
    moved = (len(refs) - 5) // 2
    sources, targets, sems = refs[:moved], refs[moved + 4 : -1], refs[-1]
    projected_ref, picker_ref, weights_ref, placed_ref = refs[moved : moved + 4]
    copies = [
        pltpu.make_async_copy(source, target, sems.at[k])
        for k, (source, target) in enumerate(zip(sources, targets))
    ]
    for copy in copies:
        copy.start()
    count = assign_ref.shape[0]
    windows, window_len = blend_ref.shape
    channels = noisy_ref.shape[-1]
    tile_pos = noisy_ref.shape[2]
    rows, low_rows = picker_ref.shape
    low_pos = low_rows // count
    own = lax.axis_index("frame")
    projected_ref[...] = dot(noisy_ref[0].reshape(rows, channels), noise_w_ref[...])
    start = starts_ref[assign_ref[own] // tiles]
    row = lax.broadcasted_iota(jnp.int32, (rows, low_rows), 0)
    column = lax.broadcasted_iota(jnp.int32, (rows, low_rows), 1)
    wanted = row // (tile_pos // low_pos) + start * low_pos
    picker_ref[...] = jnp.where(column == wanted, 1.0, 0.0).astype(BF16)
    placed_ref[...] = jnp.zeros_like(placed_ref)

    def factor_of(window):
        offset = own - starts_ref[window]
        inside = (offset >= 0) & (offset < window_len)
        clipped = jnp.clip(offset, 0, window_len - 1)
        return jnp.where(inside, blend_ref[window, clipped], 0)

    denom = lax.fori_loop(
        0, windows, lambda w, total: total + factor_of(w), jnp.int32(0), unroll=min(windows, 4)
    )
    denom_row = jnp.full((1, channels), denom, jnp.int32).astype(F32)
    weights_ref[...] = jnp.zeros_like(weights_ref)

    def body(slot, carry):
        item = assign_ref[slot]
        factor = factor_of(item // tiles)
        factor_row = jnp.full((1, channels), factor, jnp.int32).astype(F32)
        weights_ref[rank_of(slot, count), pl.ds(lax.rem(item, tiles), 1), :] = factor_row / denom_row
        return carry

    lax.fori_loop(0, count, body, 0)
    for copy in copies:
        copy.wait()


def refine_kernel(
    tiles, assign_hbm, starts_hbm, tile_ref, projected_ref, picker_ref, base_w_ref, cond_w_ref,
    gains_ref, tconv_ref, mlp_in_ref, mlp_out_ref, zeros_ref, placed_ref,
    assign_sm, starts_sm, sems,
):
    copies = [
        pltpu.make_async_copy(assign_hbm, assign_sm, sems.at[0]),
        pltpu.make_async_copy(starts_hbm, starts_sm, sems.at[1]),
    ]
    for copy in copies:
        copy.start()
    count, low_pos, channels = tile_ref.shape
    rows = projected_ref.shape[0]
    tile_pos = placed_ref.shape[1]
    window_len = rows // tile_pos
    half = count // 2
    frames = jnp.concatenate([tile_ref[half:], tile_ref[:half]], 0)
    edge = jnp.zeros((1, low_pos, channels), BF16)
    before = jnp.concatenate([edge, frames[:-1]], 0).reshape(count * low_pos, channels)
    behind = jnp.concatenate([frames[1:], edge], 0).reshape(count * low_pos, channels)
    middle = frames.reshape(count * low_pos, channels)
    total = dot(before, base_w_ref[0]) + dot(middle, base_w_ref[1]) + dot(behind, base_w_ref[2])
    base = (middle.astype(F32) + silu(total)).astype(BF16)
    cond = dot(picker_ref[...], base).astype(BF16)
    state = dot(cond, cond_w_ref[...]) + projected_ref[...]
    layers = gains_ref.shape[0]
    for layer in range(layers):
        inverse = lax.rsqrt(jnp.mean(state * state, axis=-1, keepdims=True) + 1e-06)
        normed = (state * inverse * gains_ref[layer : layer + 1, :]).reshape(
            window_len, tile_pos, channels
        )
        edge = jnp.zeros((1, tile_pos, channels), F32)
        before = jnp.concatenate([edge, normed[:-1]], 0)
        behind = jnp.concatenate([normed[1:], edge], 0)
        mixed = (
            normed
            + tconv_ref[layer, 0:1, :] * before
            + tconv_ref[layer, 1:2, :] * normed
            + tconv_ref[layer, 2:3, :] * behind
        )
        mixed = mixed.reshape(rows, channels).astype(BF16)
        pieces = []
        step = rows // CHUNKS
        for piece in range(CHUNKS):
            part = slice(piece * step, (piece + 1) * step)
            hidden = silu(dot(mixed[part], mlp_in_ref[layer])).astype(BF16)
            pieces.append(state[part] + dot(hidden, mlp_out_ref[layer]))
        state = jnp.concatenate(pieces, 0) if len(pieces) > 1 else pieces[0]
    for copy in copies:
        copy.wait()
    start = starts_sm[assign_sm[lax.axis_index("frame")] // tiles]
    refined = state.astype(BF16).reshape(window_len, tile_pos, channels)
    for frame in range(window_len):
        placed_ref[rank_of(start + frame, count)] = refined[frame]


CHUNKS = 4


def blend_kernel(received_ref, weights_ref, video_ref):
    count, tile_pos, channels = received_ref.shape
    tiles = weights_ref.shape[1]

    def body(slot, totals):
        rows = received_ref[slot].astype(F32)
        weights = weights_ref[slot]
        return tuple(totals[t] + weights[t : t + 1, :] * rows for t in range(tiles))

    zero = jnp.zeros((tile_pos, channels), F32)
    totals = lax.fori_loop(0, count, body, (zero,) * tiles, unroll=min(count, 16))
    for t in range(tiles):
        video_ref[0, t * tile_pos : (t + 1) * tile_pos, :] = totals[t].astype(BF16)


def on_device(
    lowres, noisy, starts, blend, assign, base_w, cond_w, noise_w, gains, tconv, mlp_in, mlp_out
):
    count = assign.shape[0]
    windows, window_len = blend.shape
    tiles = count // windows
    tile_pos, channels = noisy.shape[2:]
    low_pos = lowres.shape[1] // tiles
    rows = window_len * tile_pos
    hidden = mlp_in.shape[-1]
    layers = gains.shape[0]

    outgoing = pl.pallas_call(
        functools.partial(pick_kernel, tiles),
        out_shape=VMEM((count, low_pos, channels), BF16),
        in_specs=[spec(SMEM), spec(VMEM)],
        out_specs=spec(VMEM),
        compiler_params=pltpu.CompilerParams(vmem_limit_bytes=ROOM),
        name="pick",
    )(*far(assign, lowres))
    gathered = exchange(outgoing)

    moved = (base_w, cond_w, gains, tconv, mlp_in, mlp_out)
    projected, picker, weights, zeros, *params = pl.pallas_call(
        functools.partial(side_kernel, tiles),
        out_shape=(
            VMEM((rows, channels), F32),
            VMEM((rows, count * low_pos), BF16),
            VMEM((count, tiles, channels), F32),
            VMEM((count, tile_pos, channels), BF16),
            *(VMEM(array.shape, array.dtype) for array in moved),
        ),
        in_specs=[spec(SMEM)] * 3 + [spec(VMEM)] * 2 + [spec(pl.ANY)] * len(moved),
        out_specs=(spec(VMEM),) * (4 + len(moved)),
        scratch_shapes=[pltpu.SemaphoreType.DMA((len(moved),))],
        cost_estimate=pl.CostEstimate(
            flops=2 * rows * channels * channels, bytes_accessed=4 * rows * channels, transcendentals=0
        ),
        compiler_params=pltpu.CompilerParams(vmem_limit_bytes=ROOM),
        name="side",
    )(*far(assign, starts, blend, noisy, noise_w, *moved))

    placed = pl.pallas_call(
        functools.partial(refine_kernel, tiles),
        out_shape=VMEM((count, tile_pos, channels), BF16),
        in_specs=[spec(pl.ANY)] * 2 + [spec(VMEM)] * 10,
        out_specs=spec(VMEM),
        scratch_shapes=[
            SMEM(assign.shape, jnp.int32),
            SMEM(starts.shape, jnp.int32),
            pltpu.SemaphoreType.DMA((2,)),
        ],
        input_output_aliases={11: 0},
        cost_estimate=pl.CostEstimate(
            flops=4 * layers * rows * channels * hidden,
            bytes_accessed=4 * layers * channels * hidden,
            transcendentals=layers * rows * hidden,
        ),
        compiler_params=pltpu.CompilerParams(vmem_limit_bytes=ROOM),
        name="refine",
    )(
        *far(assign, starts),
        *near(gathered, projected, picker, *params, zeros),
    )
    received = exchange(placed)
    return pl.pallas_call(
        blend_kernel,
        out_shape=jax.ShapeDtypeStruct((1, tiles * tile_pos, channels), BF16),
        in_specs=[spec(VMEM)] * 2,
        out_specs=spec(VMEM),
        compiler_params=pltpu.CompilerParams(vmem_limit_bytes=ROOM),
        name="blend",
    )(*near(received, weights))


def solution(mesh):
    in_specs = (
        P(("groups", "frame"), None, None),
        P(("groups", "frame"), None, None, None),
        P("groups"),
        P("groups", None),
        P("groups"),
        P(),
        P(),
        P(),
        P(),
        P(),
        P(),
        P(),
    )
    out_specs = P(("groups", "frame"), None, None)
    return jax.shard_map(
        on_device, mesh=mesh, in_specs=in_specs, out_specs=out_specs, check_vma=False
    )
```

```python
import functools

import jax
import jax.numpy as jnp
from jax import lax
from jax.experimental import pallas as pl
from jax.experimental.pallas import tpu as pltpu
from jax.sharding import PartitionSpec as P

F32 = jnp.float32
BF16 = jnp.bfloat16
VMEM = pltpu.VMEM
SMEM = pltpu.SMEM
ROOM = 24 << 20


def dot(a, b):
    return jnp.dot(a, b, preferred_element_type=F32)


def silu(x):
    half = 0.5 * x
    return half + half * jnp.tanh(half)


def spec(space):
    return pl.BlockSpec(memory_space=space)


def near(*arrays):
    return tuple(pltpu.with_memory_space_constraint(array, VMEM) for array in arrays)


def far(*arrays):
    return tuple(pltpu.with_memory_space_constraint(array, pltpu.HBM) for array in arrays)


def rank_of(frame, count):
    return lax.rem(frame + count // 2, jnp.int32(count))


def exchange(blocks):
    count = blocks.shape[0]
    order = [(rank + count // 2) % count for rank in range(count)]
    return lax.all_to_all(
        blocks, "frame", split_axis=0, concat_axis=0, tiled=True, axis_index_groups=[order]
    )


def pick_kernel(tiles, assign_ref, low_ref, out_ref):
    count, low_pos, _ = out_ref.shape

    def body(slot, carry):
        tile = lax.rem(assign_ref[slot], tiles)
        first = pl.multiple_of(tile * low_pos, low_pos)
        out_ref[rank_of(slot, count)] = low_ref[0, pl.ds(first, low_pos), :]
        return carry

    lax.fori_loop(0, count, body, 0, unroll=min(count, 16))


def side_kernel(
    tiles, assign_ref, starts_ref, blend_ref, noisy_ref, noise_w_ref, *refs
):
    moved = (len(refs) - 5) // 2
    sources, targets, sems = refs[:moved], refs[moved + 4 : -1], refs[-1]
    projected_ref, weights_ref, placed_ref, start_ref = refs[moved : moved + 4]
    copies = [
        pltpu.make_async_copy(source, target, sems.at[k])
        for k, (source, target) in enumerate(zip(sources, targets))
    ]
    for copy in copies:
        copy.start()
    count = assign_ref.shape[0]
    windows, window_len = blend_ref.shape
    channels = noisy_ref.shape[-1]
    tile_pos = noisy_ref.shape[2]
    rows = projected_ref.shape[0]
    own = lax.axis_index("frame")
    projected_ref[...] = dot(noisy_ref[0].reshape(rows, channels), noise_w_ref[...])
    start_ref[0] = starts_ref[assign_ref[own] // tiles]
    placed_ref[...] = jnp.zeros_like(placed_ref)

    def factor_of(window):
        offset = own - starts_ref[window]
        inside = (offset >= 0) & (offset < window_len)
        clipped = jnp.clip(offset, 0, window_len - 1)
        return jnp.where(inside, blend_ref[window, clipped], 0)

    denom = lax.fori_loop(
        0, windows, lambda w, total: total + factor_of(w), jnp.int32(0), unroll=min(windows, 4)
    )
    denom_row = jnp.full((1, channels), denom, jnp.int32).astype(F32)
    weights_ref[...] = jnp.zeros_like(weights_ref)

    def body(slot, carry):
        item = assign_ref[slot]
        factor = factor_of(item // tiles)
        factor_row = jnp.full((1, channels), factor, jnp.int32).astype(F32)
        weights_ref[rank_of(slot, count), pl.ds(lax.rem(item, tiles), 1), :] = factor_row / denom_row
        return carry

    lax.fori_loop(0, count, body, 0)
    for copy in copies:
        copy.wait()


def refine_kernel(
    start_ref, tile_ref, projected_ref, base_w_ref, cond_w_ref, gains_ref, tconv_ref, mlp_in_ref,
    mlp_out_ref, zeros_ref, placed_ref, state_ref,
):
    count, low_pos, channels = tile_ref.shape
    rows = projected_ref.shape[0]
    tile_pos = placed_ref.shape[1]
    window_len = rows // tile_pos
    low_rows = window_len * low_pos
    start = start_ref[0]

    def low_frame(frame):
        inside = (frame >= 0) & (frame < count)
        rank = rank_of(jnp.clip(frame, 0, count - 1), count)
        return jnp.where(inside, tile_ref[rank], jnp.zeros((low_pos, channels), BF16))

    frames = [low_frame(start + k - 1) for k in range(window_len + 2)]
    taps = base_w_ref.shape[0]
    shifted = [jnp.concatenate(frames[k : k + window_len], 0) for k in range(taps)]
    total = dot(
        jnp.concatenate(shifted, 1), base_w_ref[...].reshape(taps * channels, channels)
    )
    base = (shifted[1].astype(F32) + silu(total)).astype(BF16)
    cond = dot(base, cond_w_ref[...])
    ratio = tile_pos // low_pos
    for k in range(ratio):
        state_ref[pl.ds(k, low_rows, stride=ratio), :] = cond
    state = state_ref[...] + projected_ref[...]
    for layer in range(gains_ref.shape[0]):
        inverse = lax.rsqrt(jnp.mean(state * state, axis=-1, keepdims=True) + 1e-06)
        scaled = state * inverse
        gain = gains_ref[layer : layer + 1, :]
        previous, same, following = (
            gain * tconv_ref[layer, 0:1, :],
            gain * (1.0 + tconv_ref[layer, 1:2, :]),
            gain * tconv_ref[layer, 2:3, :],
        )
        block = [scaled[k * tile_pos : (k + 1) * tile_pos] for k in range(window_len)]
        parts = []
        for k in range(window_len):
            mixed = same * block[k]
            if k > 0:
                mixed = mixed + previous * block[k - 1]
            if k + 1 < window_len:
                mixed = mixed + following * block[k + 1]
            parts.append(mixed.astype(BF16))
        half = (0.5 * dot(jnp.concatenate(parts, 0), mlp_in_ref[layer])).astype(BF16)
        hidden = half + half * jnp.tanh(half)
        state = state + dot(hidden, mlp_out_ref[layer])
    refined = state.astype(BF16).reshape(window_len, tile_pos, channels)
    for frame in range(window_len):
        placed_ref[rank_of(start + frame, count)] = refined[frame]


def blend_kernel(received_ref, weights_ref, video_ref):
    count, tile_pos, channels = received_ref.shape
    tiles = weights_ref.shape[1]

    def body(slot, totals):
        rows = received_ref[slot].astype(F32)
        weights = weights_ref[slot]
        return tuple(totals[t] + weights[t : t + 1, :] * rows for t in range(tiles))

    zero = jnp.zeros((tile_pos, channels), F32)
    totals = lax.fori_loop(0, count, body, (zero,) * tiles, unroll=min(count, 16))
    for t in range(tiles):
        video_ref[0, t * tile_pos : (t + 1) * tile_pos, :] = totals[t].astype(BF16)


def on_device(
    lowres, noisy, starts, blend, assign, base_w, cond_w, noise_w, gains, tconv, mlp_in, mlp_out
):
    count = assign.shape[0]
    windows, window_len = blend.shape
    tiles = count // windows
    tile_pos, channels = noisy.shape[2:]
    low_pos = lowres.shape[1] // tiles
    rows = window_len * tile_pos
    hidden = mlp_in.shape[-1]
    layers = gains.shape[0]

    outgoing = pl.pallas_call(
        functools.partial(pick_kernel, tiles),
        out_shape=VMEM((count, low_pos, channels), BF16),
        in_specs=[spec(SMEM), spec(VMEM)],
        out_specs=spec(VMEM),
        compiler_params=pltpu.CompilerParams(vmem_limit_bytes=ROOM),
        name="pick",
    )(*far(assign, lowres))
    gathered = exchange(outgoing)

    moved = (base_w, cond_w, gains, tconv, mlp_in, mlp_out)
    projected, weights, zeros, first, *params = pl.pallas_call(
        functools.partial(side_kernel, tiles),
        out_shape=(
            VMEM((rows, channels), F32),
            VMEM((count, tiles, channels), F32),
            VMEM((count, tile_pos, channels), BF16),
            SMEM((1,), jnp.int32),
            *(VMEM(array.shape, array.dtype) for array in moved),
        ),
        in_specs=[spec(SMEM)] * 3 + [spec(VMEM)] * 2 + [spec(pl.ANY)] * len(moved),
        out_specs=(*(spec(VMEM),) * 3, spec(SMEM), *(spec(VMEM),) * len(moved)),
        scratch_shapes=[pltpu.SemaphoreType.DMA((len(moved),))],
        cost_estimate=pl.CostEstimate(
            flops=2 * rows * channels * channels, bytes_accessed=4 * rows * channels, transcendentals=0
        ),
        compiler_params=pltpu.CompilerParams(vmem_limit_bytes=ROOM),
        name="side",
    )(*far(assign, starts, blend, noisy, noise_w, *moved))

    placed = pl.pallas_call(
        refine_kernel,
        out_shape=VMEM((count, tile_pos, channels), BF16),
        in_specs=[spec(SMEM)] + [spec(VMEM)] * 9,
        out_specs=spec(VMEM),
        scratch_shapes=[VMEM((rows, channels), F32)],
        input_output_aliases={9: 0},
        cost_estimate=pl.CostEstimate(
            flops=4 * layers * rows * channels * hidden,
            bytes_accessed=4 * layers * channels * hidden,
            transcendentals=layers * rows * hidden,
        ),
        compiler_params=pltpu.CompilerParams(vmem_limit_bytes=ROOM),
        name="refine",
    )(
        first,
        *near(gathered, projected, *params, zeros),
    )
    received = exchange(placed)
    return pl.pallas_call(
        blend_kernel,
        out_shape=jax.ShapeDtypeStruct((1, tiles * tile_pos, channels), BF16),
        in_specs=[spec(VMEM)] * 2,
        out_specs=spec(VMEM),
        compiler_params=pltpu.CompilerParams(vmem_limit_bytes=ROOM),
        name="blend",
    )(*near(received, weights))


def solution(mesh):
    in_specs = (
        P(("groups", "frame"), None, None),
        P(("groups", "frame"), None, None, None),
        P("groups"),
        P("groups", None),
        P("groups"),
        P(),
        P(),
        P(),
        P(),
        P(),
        P(),
        P(),
    )
    out_specs = P(("groups", "frame"), None, None)
    return jax.shard_map(
        on_device, mesh=mesh, in_specs=in_specs, out_specs=out_specs, check_vma=False
    )
```

```python
import functools

import jax
import jax.numpy as jnp
from jax import lax
from jax.experimental import pallas as pl
from jax.experimental.pallas import tpu as pltpu
from jax.sharding import PartitionSpec as P

F32 = jnp.float32
BF16 = jnp.bfloat16
VMEM = pltpu.VMEM
SMEM = pltpu.SMEM
ROOM = 24 << 20


def dot(a, b):
    return jnp.dot(a, b, preferred_element_type=F32)


def silu(x):
    half = 0.5 * x
    return half + half * jnp.tanh(half)


def spec(space):
    return pl.BlockSpec(memory_space=space)


def near(*arrays):
    return tuple(pltpu.with_memory_space_constraint(array, VMEM) for array in arrays)


def far(*arrays):
    return tuple(pltpu.with_memory_space_constraint(array, pltpu.HBM) for array in arrays)


FIRST = (2, 0, 1, 3)
SECOND = (2, 0, 1, 3)


def rank_of(frame, count, quarters):
    quarter = count // 4
    block, rest = frame // quarter, lax.rem(frame, quarter)
    place = sum(jnp.where(block == q, spot, 0) for spot, q in enumerate(quarters))
    return place * quarter + quarter - 1 - rest


def exchange(blocks, quarters):
    count = blocks.shape[0]
    quarter = count // 4
    order = [q * quarter + k for q in quarters for k in reversed(range(quarter))]
    return lax.all_to_all(
        blocks, "frame", split_axis=0, concat_axis=0, tiled=True, axis_index_groups=[order]
    )


def pick_kernel(tiles, assign_ref, low_ref, out_ref):
    count, low_pos, _ = out_ref.shape

    def body(slot, carry):
        tile = lax.rem(assign_ref[slot], tiles)
        first = pl.multiple_of(tile * low_pos, low_pos)
        out_ref[rank_of(slot, count, FIRST)] = low_ref[0, pl.ds(first, low_pos), :]
        return carry

    lax.fori_loop(0, count, body, 0, unroll=min(count, 16))


def side_kernel(
    tiles, assign_ref, starts_ref, blend_ref, noisy_ref, noise_w_ref, *refs
):
    moved = (len(refs) - 5) // 2
    sources, targets, sems = refs[:moved], refs[moved + 4 : -1], refs[-1]
    projected_ref, weights_ref, placed_ref, spots_ref = refs[moved : moved + 4]
    copies = [
        pltpu.make_async_copy(source, target, sems.at[k])
        for k, (source, target) in enumerate(zip(sources, targets))
    ]
    for copy in copies:
        copy.start()
    count = assign_ref.shape[0]
    windows, window_len = blend_ref.shape
    channels = noisy_ref.shape[-1]
    tile_pos = noisy_ref.shape[2]
    rows = projected_ref.shape[0]
    own = lax.axis_index("frame")
    projected_ref[...] = dot(noisy_ref[0].reshape(rows, channels), noise_w_ref[...])
    start = starts_ref[assign_ref[own] // tiles]
    for k in range(window_len + 2):
        frame = start + k - 1
        inside = (frame >= 0) & (frame < count)
        near_frame = jnp.clip(frame, 0, count - 1)
        spots_ref[k] = jnp.where(inside, rank_of(near_frame, count, FIRST), -1)
        spots_ref[window_len + 2 + k] = rank_of(near_frame, count, SECOND)
    placed_ref[...] = jnp.zeros_like(placed_ref)

    def factor_of(window):
        offset = own - starts_ref[window]
        inside = (offset >= 0) & (offset < window_len)
        clipped = jnp.clip(offset, 0, window_len - 1)
        return jnp.where(inside, blend_ref[window, clipped], 0)

    denom = lax.fori_loop(
        0, windows, lambda w, total: total + factor_of(w), jnp.int32(0), unroll=min(windows, 4)
    )
    denom_row = jnp.full((1, channels), denom, jnp.int32).astype(F32)
    weights_ref[...] = jnp.zeros_like(weights_ref)

    def body(slot, carry):
        item = assign_ref[slot]
        factor = factor_of(item // tiles)
        factor_row = jnp.full((1, channels), factor, jnp.int32).astype(F32)
        spot = rank_of(slot, count, SECOND)
        weights_ref[spot, pl.ds(lax.rem(item, tiles), 1), :] = factor_row / denom_row
        return carry

    lax.fori_loop(0, count, body, 0)
    for copy in copies:
        copy.wait()


def refine_kernel(
    spots_ref, tile_ref, projected_ref, base_w_ref, cond_w_ref, gains_ref, tconv_ref, mlp_in_ref,
    mlp_out_ref, zeros_ref, placed_ref, state_ref,
):
    _, low_pos, channels = tile_ref.shape
    rows = projected_ref.shape[0]
    tile_pos = placed_ref.shape[1]
    window_len = rows // tile_pos
    low_rows = window_len * low_pos

    def low_frame(k):
        spot = spots_ref[k]
        frame = tile_ref[jnp.maximum(spot, 0)]
        if 0 < k <= window_len:
            return frame
        return jnp.where(spot >= 0, frame, jnp.zeros_like(frame))

    frames = [low_frame(k) for k in range(window_len + 2)]
    taps = base_w_ref.shape[0]
    shifted = [jnp.concatenate(frames[k : k + window_len], 0) for k in range(taps)]
    total = dot(
        jnp.concatenate(shifted, 1), base_w_ref[...].reshape(taps * channels, channels)
    )
    base = (shifted[1].astype(F32) + silu(total)).astype(BF16)
    cond = dot(base, cond_w_ref[...])
    ratio = tile_pos // low_pos
    for k in range(ratio):
        state_ref[pl.ds(k, low_rows, stride=ratio), :] = cond
    state = state_ref[...] + projected_ref[...]
    for layer in range(gains_ref.shape[0]):
        inverse = lax.rsqrt(jnp.mean(state * state, axis=-1, keepdims=True) + 1e-06)
        scaled = state * inverse
        gain = gains_ref[layer : layer + 1, :]
        previous, same, following = (
            gain * tconv_ref[layer, 0:1, :],
            gain * (1.0 + tconv_ref[layer, 1:2, :]),
            gain * tconv_ref[layer, 2:3, :],
        )
        block = [scaled[k * tile_pos : (k + 1) * tile_pos] for k in range(window_len)]
        parts = []
        for k in range(window_len):
            mixed = same * block[k]
            if k > 0:
                mixed = mixed + previous * block[k - 1]
            if k + 1 < window_len:
                mixed = mixed + following * block[k + 1]
            parts.append(mixed.astype(BF16))
        half = (0.5 * dot(jnp.concatenate(parts, 0), mlp_in_ref[layer])).astype(BF16)
        hidden = half + half * jnp.tanh(half)
        state = state + dot(hidden, mlp_out_ref[layer])
    refined = state.astype(BF16).reshape(window_len, tile_pos, channels)
    for frame in range(window_len):
        placed_ref[spots_ref[window_len + 3 + frame]] = refined[frame]


def blend_kernel(received_ref, weights_ref, video_ref):
    count, tile_pos, channels = received_ref.shape
    tiles = weights_ref.shape[1]

    def body(slot, totals):
        rows = received_ref[slot].astype(F32)
        weights = weights_ref[slot]
        return tuple(totals[t] + weights[t : t + 1, :] * rows for t in range(tiles))

    zero = jnp.zeros((tile_pos, channels), F32)
    totals = lax.fori_loop(0, count, body, (zero,) * tiles, unroll=min(count, 16))
    for t in range(tiles):
        video_ref[0, t * tile_pos : (t + 1) * tile_pos, :] = totals[t].astype(BF16)


def on_device(
    lowres, noisy, starts, blend, assign, base_w, cond_w, noise_w, gains, tconv, mlp_in, mlp_out
):
    count = assign.shape[0]
    windows, window_len = blend.shape
    tiles = count // windows
    tile_pos, channels = noisy.shape[2:]
    low_pos = lowres.shape[1] // tiles
    rows = window_len * tile_pos
    hidden = mlp_in.shape[-1]
    layers = gains.shape[0]

    outgoing = pl.pallas_call(
        functools.partial(pick_kernel, tiles),
        out_shape=VMEM((count, low_pos, channels), BF16),
        in_specs=[spec(SMEM), spec(VMEM)],
        out_specs=spec(VMEM),
        compiler_params=pltpu.CompilerParams(vmem_limit_bytes=ROOM),
        name="pick",
    )(*far(assign, lowres))
    gathered = exchange(outgoing, FIRST)

    moved = (base_w, cond_w, gains, tconv, mlp_in, mlp_out)
    projected, weights, zeros, spots, *params = pl.pallas_call(
        functools.partial(side_kernel, tiles),
        out_shape=(
            VMEM((rows, channels), F32),
            VMEM((count, tiles, channels), F32),
            VMEM((count, tile_pos, channels), BF16),
            SMEM((2 * (window_len + 2),), jnp.int32),
            *(VMEM(array.shape, array.dtype) for array in moved),
        ),
        in_specs=[spec(SMEM)] * 3 + [spec(VMEM)] * 2 + [spec(pl.ANY)] * len(moved),
        out_specs=(*(spec(VMEM),) * 3, spec(SMEM), *(spec(VMEM),) * len(moved)),
        scratch_shapes=[pltpu.SemaphoreType.DMA((len(moved),))],
        cost_estimate=pl.CostEstimate(
            flops=2 * rows * channels * channels, bytes_accessed=4 * rows * channels, transcendentals=0
        ),
        compiler_params=pltpu.CompilerParams(vmem_limit_bytes=ROOM),
        name="side",
    )(*far(assign, starts, blend, noisy, noise_w, *moved))

    placed = pl.pallas_call(
        refine_kernel,
        out_shape=VMEM((count, tile_pos, channels), BF16),
        in_specs=[spec(SMEM)] + [spec(VMEM)] * 9,
        out_specs=spec(VMEM),
        scratch_shapes=[VMEM((rows, channels), F32)],
        input_output_aliases={9: 0},
        cost_estimate=pl.CostEstimate(
            flops=4 * layers * rows * channels * hidden,
            bytes_accessed=4 * layers * channels * hidden,
            transcendentals=layers * rows * hidden,
        ),
        compiler_params=pltpu.CompilerParams(vmem_limit_bytes=ROOM),
        name="refine",
    )(
        spots,
        *near(gathered, projected, *params, zeros),
    )
    received = exchange(placed, SECOND)
    return pl.pallas_call(
        blend_kernel,
        out_shape=jax.ShapeDtypeStruct((1, tiles * tile_pos, channels), BF16),
        in_specs=[spec(VMEM)] * 2,
        out_specs=spec(VMEM),
        compiler_params=pltpu.CompilerParams(vmem_limit_bytes=ROOM),
        name="blend",
    )(*near(received, weights))


def solution(mesh):
    in_specs = (
        P(("groups", "frame"), None, None),
        P(("groups", "frame"), None, None, None),
        P("groups"),
        P("groups", None),
        P("groups"),
        P(),
        P(),
        P(),
        P(),
        P(),
        P(),
        P(),
    )
    out_specs = P(("groups", "frame"), None, None)
    return jax.shard_map(
        on_device, mesh=mesh, in_specs=in_specs, out_specs=out_specs, check_vma=False
    )
```

```python
import functools

import jax
import jax.numpy as jnp
from jax import lax
from jax.experimental import pallas as pl
from jax.experimental.pallas import tpu as pltpu
from jax.sharding import PartitionSpec as P

F32 = jnp.float32
BF16 = jnp.bfloat16
VMEM = pltpu.VMEM
SMEM = pltpu.SMEM
ROOM = 24 << 20


def dot(a, b):
    return jnp.dot(a, b, preferred_element_type=F32)


def silu(x):
    half = 0.5 * x
    return half + half * jnp.tanh(half)


def spec(space):
    return pl.BlockSpec(memory_space=space)


def near(*arrays):
    return tuple(pltpu.with_memory_space_constraint(array, VMEM) for array in arrays)


def far(*arrays):
    return tuple(pltpu.with_memory_space_constraint(array, pltpu.HBM) for array in arrays)


FIRST = (11, 10, 9, 8, 3, 2, 1, 0, 7, 6, 5, 4, 15, 14, 13, 12)
SECOND = (11, 10, 9, 8, 13, 6, 1, 0, 7, 12, 5, 4, 15, 3, 2, 14)


def order_of(count, cells):
    width = count // len(cells)
    if width * len(cells) != count:
        return list(range(count))
    return [cell * width + k for cell in cells for k in range(width)]


def ranks_of(count, cells):
    order = order_of(count, cells)
    return [order.index(frame) for frame in range(count)]


def exchange(blocks, cells):
    order = order_of(blocks.shape[0], cells)
    return lax.all_to_all(
        blocks, "frame", split_axis=0, concat_axis=0, tiled=True, axis_index_groups=[order]
    )


def pick_kernel(tiles, assign_ref, low_ref, out_ref):
    count, low_pos, _ = out_ref.shape
    for slot, rank in enumerate(ranks_of(count, FIRST)):
        tile = lax.rem(assign_ref[slot], tiles)
        first = pl.multiple_of(tile * low_pos, low_pos)
        out_ref[rank] = low_ref[0, pl.ds(first, low_pos), :]


def side_kernel(
    tiles, assign_ref, starts_ref, blend_ref, noisy_ref, noise_w_ref, *refs
):
    moved = (len(refs) - 6) // 2
    sources, targets, ranks_ref, sems = refs[:moved], refs[moved + 4 : -2], refs[-2], refs[-1]
    projected_ref, weights_ref, placed_ref, spots_ref = refs[moved : moved + 4]
    copies = [
        pltpu.make_async_copy(source, target, sems.at[k])
        for k, (source, target) in enumerate(zip(sources, targets))
    ]
    for copy in copies:
        copy.start()
    count = assign_ref.shape[0]
    windows, window_len = blend_ref.shape
    channels = noisy_ref.shape[-1]
    tile_pos = noisy_ref.shape[2]
    rows = projected_ref.shape[0]
    own = lax.axis_index("frame")
    projected_ref[...] = dot(noisy_ref[0].reshape(rows, channels), noise_w_ref[...])
    for side, cells in enumerate((FIRST, SECOND)):
        for frame, rank in enumerate(ranks_of(count, cells)):
            ranks_ref[side * count + frame] = rank
    start = starts_ref[assign_ref[own] // tiles]
    for k in range(window_len + 2):
        frame = start + k - 1
        inside = (frame >= 0) & (frame < count)
        near_frame = jnp.clip(frame, 0, count - 1)
        spots_ref[k] = jnp.where(inside, ranks_ref[near_frame], -1)
        spots_ref[window_len + 2 + k] = ranks_ref[count + near_frame]
    placed_ref[...] = jnp.zeros_like(placed_ref)

    def factor_of(window):
        offset = own - starts_ref[window]
        inside = (offset >= 0) & (offset < window_len)
        clipped = jnp.clip(offset, 0, window_len - 1)
        return jnp.where(inside, blend_ref[window, clipped], 0)

    denom = lax.fori_loop(
        0, windows, lambda w, total: total + factor_of(w), jnp.int32(0), unroll=min(windows, 4)
    )
    denom_row = jnp.full((1, channels), denom, jnp.int32).astype(F32)
    weights_ref[...] = jnp.zeros_like(weights_ref)

    def body(slot, carry):
        item = assign_ref[slot]
        factor = factor_of(item // tiles)
        factor_row = jnp.full((1, channels), factor, jnp.int32).astype(F32)
        spot = ranks_ref[count + slot]
        weights_ref[spot, pl.ds(lax.rem(item, tiles), 1), :] = factor_row / denom_row
        return carry

    lax.fori_loop(0, count, body, 0)
    for copy in copies:
        copy.wait()


def refine_kernel(
    spots_ref, tile_ref, projected_ref, base_w_ref, cond_w_ref, gains_ref, tconv_ref, mlp_in_ref,
    mlp_out_ref, zeros_ref, placed_ref, state_ref,
):
    _, low_pos, channels = tile_ref.shape
    rows = projected_ref.shape[0]
    tile_pos = placed_ref.shape[1]
    window_len = rows // tile_pos
    low_rows = window_len * low_pos

    def low_frame(k):
        spot = spots_ref[k]
        frame = tile_ref[jnp.maximum(spot, 0)]
        if 0 < k <= window_len:
            return frame
        return jnp.where(spot >= 0, frame, jnp.zeros_like(frame))

    frames = [low_frame(k) for k in range(window_len + 2)]
    taps = base_w_ref.shape[0]
    shifted = [jnp.concatenate(frames[k : k + window_len], 0) for k in range(taps)]
    total = dot(
        jnp.concatenate(shifted, 1), base_w_ref[...].reshape(taps * channels, channels)
    )
    base = (shifted[1].astype(F32) + silu(total)).astype(BF16)
    cond = dot(base, cond_w_ref[...])
    ratio = tile_pos // low_pos
    for k in range(ratio):
        state_ref[pl.ds(k, low_rows, stride=ratio), :] = cond
    state = state_ref[...] + projected_ref[...]
    for layer in range(gains_ref.shape[0]):
        inverse = lax.rsqrt(jnp.mean(state * state, axis=-1, keepdims=True) + 1e-06)
        scaled = state * inverse
        gain = 0.5 * gains_ref[layer : layer + 1, :]
        previous, same, following = (
            gain * tconv_ref[layer, 0:1, :],
            gain * (1.0 + tconv_ref[layer, 1:2, :]),
            gain * tconv_ref[layer, 2:3, :],
        )
        block = [scaled[k * tile_pos : (k + 1) * tile_pos] for k in range(window_len)]
        parts = []
        for k in range(window_len):
            mixed = same * block[k]
            if k > 0:
                mixed = mixed + previous * block[k - 1]
            if k + 1 < window_len:
                mixed = mixed + following * block[k + 1]
            parts.append(mixed.astype(BF16))
        half = dot(jnp.concatenate(parts, 0), mlp_in_ref[layer])
        hidden = (half + half * jnp.tanh(half)).astype(BF16)
        state = state + dot(hidden, mlp_out_ref[layer])
    refined = state.astype(BF16).reshape(window_len, tile_pos, channels)
    for frame in range(window_len):
        placed_ref[spots_ref[window_len + 3 + frame]] = refined[frame]


def blend_kernel(received_ref, weights_ref, video_ref):
    count, tile_pos, channels = received_ref.shape
    tiles = weights_ref.shape[1]

    def body(slot, totals):
        rows = received_ref[slot].astype(F32)
        weights = weights_ref[slot]
        return tuple(totals[t] + weights[t : t + 1, :] * rows for t in range(tiles))

    zero = jnp.zeros((tile_pos, channels), F32)
    totals = lax.fori_loop(0, count, body, (zero,) * tiles, unroll=min(count, 16))
    for t in range(tiles):
        video_ref[0, t * tile_pos : (t + 1) * tile_pos, :] = totals[t].astype(BF16)


def on_device(
    lowres, noisy, starts, blend, assign, base_w, cond_w, noise_w, gains, tconv, mlp_in, mlp_out
):
    count = assign.shape[0]
    windows, window_len = blend.shape
    tiles = count // windows
    tile_pos, channels = noisy.shape[2:]
    low_pos = lowres.shape[1] // tiles
    rows = window_len * tile_pos
    hidden = mlp_in.shape[-1]
    layers = gains.shape[0]

    outgoing = pl.pallas_call(
        functools.partial(pick_kernel, tiles),
        out_shape=VMEM((count, low_pos, channels), BF16),
        in_specs=[spec(SMEM), spec(VMEM)],
        out_specs=spec(VMEM),
        compiler_params=pltpu.CompilerParams(vmem_limit_bytes=ROOM),
        name="pick",
    )(*far(assign, lowres))
    gathered = exchange(outgoing, FIRST)

    moved = (base_w, cond_w, gains, tconv, mlp_in, mlp_out)
    projected, weights, zeros, spots, *params = pl.pallas_call(
        functools.partial(side_kernel, tiles),
        out_shape=(
            VMEM((rows, channels), F32),
            VMEM((count, tiles, channels), F32),
            VMEM((count, tile_pos, channels), BF16),
            SMEM((2 * (window_len + 2),), jnp.int32),
            *(VMEM(array.shape, array.dtype) for array in moved),
        ),
        in_specs=[spec(SMEM)] * 3 + [spec(VMEM)] * 2 + [spec(pl.ANY)] * len(moved),
        out_specs=(*(spec(VMEM),) * 3, spec(SMEM), *(spec(VMEM),) * len(moved)),
        scratch_shapes=[
            SMEM((2 * count,), jnp.int32),
            pltpu.SemaphoreType.DMA((len(moved),)),
        ],
        cost_estimate=pl.CostEstimate(
            flops=2 * rows * channels * channels, bytes_accessed=4 * rows * channels, transcendentals=0
        ),
        compiler_params=pltpu.CompilerParams(vmem_limit_bytes=ROOM),
        name="side",
    )(*far(assign, starts, blend, noisy, noise_w, *moved))

    placed = pl.pallas_call(
        refine_kernel,
        out_shape=VMEM((count, tile_pos, channels), BF16),
        in_specs=[spec(SMEM)] + [spec(VMEM)] * 9,
        out_specs=spec(VMEM),
        scratch_shapes=[VMEM((rows, channels), F32)],
        input_output_aliases={9: 0},
        cost_estimate=pl.CostEstimate(
            flops=4 * layers * rows * channels * hidden,
            bytes_accessed=4 * layers * channels * hidden,
            transcendentals=layers * rows * hidden,
        ),
        compiler_params=pltpu.CompilerParams(vmem_limit_bytes=ROOM),
        name="refine",
    )(
        spots,
        *near(gathered, projected, *params, zeros),
    )
    received = exchange(placed, SECOND)
    return pl.pallas_call(
        blend_kernel,
        out_shape=jax.ShapeDtypeStruct((1, tiles * tile_pos, channels), BF16),
        in_specs=[spec(VMEM)] * 2,
        out_specs=spec(VMEM),
        compiler_params=pltpu.CompilerParams(vmem_limit_bytes=ROOM),
        name="blend",
    )(*near(received, weights))


def solution(mesh):
    in_specs = (
        P(("groups", "frame"), None, None),
        P(("groups", "frame"), None, None, None),
        P("groups"),
        P("groups", None),
        P("groups"),
        P(),
        P(),
        P(),
        P(),
        P(),
        P(),
        P(),
    )
    out_specs = P(("groups", "frame"), None, None)
    return jax.shard_map(
        on_device, mesh=mesh, in_specs=in_specs, out_specs=out_specs, check_vma=False
    )
```

```python
import functools

import jax
import jax.numpy as jnp
from jax import lax
from jax.experimental import pallas as pl
from jax.experimental.pallas import tpu as pltpu
from jax.sharding import PartitionSpec as P

F32 = jnp.float32
BF16 = jnp.bfloat16
VMEM = pltpu.VMEM
SMEM = pltpu.SMEM
ROOM = 24 << 20


def dot(a, b):
    return jnp.dot(a, b, preferred_element_type=F32)


def silu(x):
    half = 0.5 * x
    return half + half * jnp.tanh(half)


def spec(space):
    return pl.BlockSpec(memory_space=space)


def near(*arrays):
    return tuple(pltpu.with_memory_space_constraint(array, VMEM) for array in arrays)


def far(*arrays):
    return tuple(pltpu.with_memory_space_constraint(array, pltpu.HBM) for array in arrays)


FIRST = (11, 10, 9, 8, 3, 2, 1, 0, 7, 6, 5, 4, 15, 14, 13, 12)
SECOND = (11, 10, 4, 8, 13, 6, 15, 0, 7, 1, 5, 12, 9, 3, 2, 14)


def order_of(count, cells):
    width = count // len(cells)
    if width * len(cells) != count:
        return list(range(count))
    return [cell * width + k for cell in cells for k in range(width)]


def ranks_of(count, cells):
    order = order_of(count, cells)
    return [order.index(frame) for frame in range(count)]


def exchange(blocks, cells):
    order = order_of(blocks.shape[0], cells)
    return lax.all_to_all(
        blocks, "frame", split_axis=0, concat_axis=0, tiled=True, axis_index_groups=[order]
    )


def pick_kernel(tiles, assign_ref, low_ref, out_ref):
    count, low_pos, _ = out_ref.shape
    for slot, rank in enumerate(ranks_of(count, FIRST)):
        tile = lax.rem(assign_ref[slot], tiles)
        first = pl.multiple_of(tile * low_pos, low_pos)
        out_ref[rank] = low_ref[0, pl.ds(first, low_pos), :]


def side_kernel(
    tiles, assign_ref, starts_ref, blend_ref, noisy_ref, noise_w_ref, *refs
):
    moved = (len(refs) - 6) // 2
    sources, targets, ranks_ref, sems = refs[:moved], refs[moved + 4 : -2], refs[-2], refs[-1]
    projected_ref, weights_ref, placed_ref, spots_ref = refs[moved : moved + 4]
    copies = [
        pltpu.make_async_copy(source, target, sems.at[k])
        for k, (source, target) in enumerate(zip(sources, targets))
    ]
    for copy in copies:
        copy.start()
    count = assign_ref.shape[0]
    windows, window_len = blend_ref.shape
    channels = noisy_ref.shape[-1]
    tile_pos = noisy_ref.shape[2]
    rows = projected_ref.shape[0]
    own = lax.axis_index("frame")
    projected_ref[...] = dot(noisy_ref[0].reshape(rows, channels), noise_w_ref[...])
    for side, cells in enumerate((FIRST, SECOND)):
        for frame, rank in enumerate(ranks_of(count, cells)):
            ranks_ref[side * count + frame] = rank
    start = starts_ref[assign_ref[own] // tiles]
    for k in range(window_len + 2):
        frame = start + k - 1
        inside = (frame >= 0) & (frame < count)
        near_frame = jnp.clip(frame, 0, count - 1)
        spots_ref[k] = jnp.where(inside, ranks_ref[near_frame], -1)
        spots_ref[window_len + 2 + k] = ranks_ref[count + near_frame]
    placed_ref[...] = jnp.zeros_like(placed_ref)

    def factor_of(window):
        offset = own - starts_ref[window]
        inside = (offset >= 0) & (offset < window_len)
        clipped = jnp.clip(offset, 0, window_len - 1)
        return jnp.where(inside, blend_ref[window, clipped], 0)

    denom = lax.fori_loop(
        0, windows, lambda w, total: total + factor_of(w), jnp.int32(0), unroll=min(windows, 4)
    )
    denom_row = jnp.full((1, channels), denom, jnp.int32).astype(F32)
    weights_ref[...] = jnp.zeros_like(weights_ref)

    def body(slot, carry):
        item = assign_ref[slot]
        factor = factor_of(item // tiles)
        factor_row = jnp.full((1, channels), factor, jnp.int32).astype(F32)
        spot = ranks_ref[count + slot]
        weights_ref[spot, pl.ds(lax.rem(item, tiles), 1), :] = factor_row / denom_row
        return carry

    lax.fori_loop(0, count, body, 0)
    for copy in copies:
        copy.wait()


def refine_kernel(
    spots_ref, tile_ref, projected_ref, base_w_ref, cond_w_ref, gains_ref, tconv_ref, mlp_in_ref,
    mlp_out_ref, zeros_ref, placed_ref, state_ref,
):
    _, low_pos, channels = tile_ref.shape
    rows = projected_ref.shape[0]
    tile_pos = placed_ref.shape[1]
    window_len = rows // tile_pos
    low_rows = window_len * low_pos

    def low_frame(k):
        spot = spots_ref[k]
        frame = tile_ref[jnp.maximum(spot, 0)]
        if 0 < k <= window_len:
            return frame
        return jnp.where(spot >= 0, frame, jnp.zeros_like(frame))

    frames = [low_frame(k) for k in range(window_len + 2)]
    taps = base_w_ref.shape[0]
    shifted = [jnp.concatenate(frames[k : k + window_len], 0) for k in range(taps)]
    total = dot(
        jnp.concatenate(shifted, 1), base_w_ref[...].reshape(taps * channels, channels)
    )
    base = (shifted[1].astype(F32) + silu(total)).astype(BF16)
    cond = dot(base, cond_w_ref[...])
    ratio = tile_pos // low_pos
    for k in range(ratio):
        state_ref[pl.ds(k, low_rows, stride=ratio), :] = cond
    state = state_ref[:rows] + projected_ref[...]
    for layer in range(gains_ref.shape[0]):
        inverse = lax.rsqrt(jnp.mean(state * state, axis=-1, keepdims=True) + 1e-06)
        scaled = state * inverse
        gain = 0.5 * gains_ref[layer : layer + 1, :]
        previous, same, following = (
            gain * tconv_ref[layer, 0:1, :],
            gain * (1.0 + tconv_ref[layer, 1:2, :]),
            gain * tconv_ref[layer, 2:3, :],
        )
        block = [scaled[k * tile_pos : (k + 1) * tile_pos] for k in range(window_len)]
        parts = []
        for k in range(window_len):
            mixed = same * block[k]
            if k > 0:
                mixed = mixed + previous * block[k - 1]
            if k + 1 < window_len:
                mixed = mixed + following * block[k + 1]
            parts.append(mixed.astype(BF16))
        half = dot(jnp.concatenate(parts, 0), mlp_in_ref[layer])
        hidden = (half + half * jnp.tanh(half)).astype(BF16)
        state = state + dot(hidden, mlp_out_ref[layer])
    refined = state.astype(BF16).reshape(window_len, tile_pos, channels)
    for frame in range(window_len):
        placed_ref[spots_ref[window_len + 3 + frame]] = refined[frame]


def blend_kernel(received_ref, weights_ref, video_ref):
    count, tile_pos, channels = received_ref.shape
    tiles = weights_ref.shape[1]

    def body(slot, totals):
        rows = received_ref[slot].astype(F32)
        weights = weights_ref[slot]
        return tuple(totals[t] + weights[t : t + 1, :] * rows for t in range(tiles))

    zero = jnp.zeros((tile_pos, channels), F32)
    totals = lax.fori_loop(0, count, body, (zero,) * tiles, unroll=min(count, 16))
    for t in range(tiles):
        video_ref[0, t * tile_pos : (t + 1) * tile_pos, :] = totals[t].astype(BF16)


def on_device(
    lowres, noisy, starts, blend, assign, base_w, cond_w, noise_w, gains, tconv, mlp_in, mlp_out
):
    count = assign.shape[0]
    windows, window_len = blend.shape
    tiles = count // windows
    tile_pos, channels = noisy.shape[2:]
    low_pos = lowres.shape[1] // tiles
    rows = window_len * tile_pos
    hidden = mlp_in.shape[-1]
    layers = gains.shape[0]

    outgoing = pl.pallas_call(
        functools.partial(pick_kernel, tiles),
        out_shape=VMEM((count, low_pos, channels), BF16),
        in_specs=[spec(SMEM), spec(VMEM)],
        out_specs=spec(VMEM),
        compiler_params=pltpu.CompilerParams(vmem_limit_bytes=ROOM),
        name="pick",
    )(*far(assign, lowres))
    gathered = exchange(outgoing, FIRST)

    moved = (base_w, cond_w, gains, tconv, mlp_in, mlp_out)
    projected, weights, zeros, spots, *params = pl.pallas_call(
        functools.partial(side_kernel, tiles),
        out_shape=(
            VMEM((rows, channels), F32),
            VMEM((count, tiles, channels), F32),
            VMEM((count, tile_pos, channels), BF16),
            SMEM((2 * (window_len + 2),), jnp.int32),
            *(VMEM(array.shape, array.dtype) for array in moved),
        ),
        in_specs=[spec(SMEM)] * 3 + [spec(VMEM)] * 2 + [spec(pl.ANY)] * len(moved),
        out_specs=(*(spec(VMEM),) * 3, spec(SMEM), *(spec(VMEM),) * len(moved)),
        scratch_shapes=[
            SMEM((2 * count,), jnp.int32),
            pltpu.SemaphoreType.DMA((len(moved),)),
        ],
        cost_estimate=pl.CostEstimate(
            flops=2 * rows * channels * channels, bytes_accessed=4 * rows * channels, transcendentals=0
        ),
        compiler_params=pltpu.CompilerParams(vmem_limit_bytes=ROOM),
        name="side",
    )(*far(assign, starts, blend, noisy, noise_w, *moved))

    placed = pl.pallas_call(
        refine_kernel,
        out_shape=VMEM((count, tile_pos, channels), BF16),
        in_specs=[spec(SMEM)] + [spec(VMEM)] * 9,
        out_specs=spec(VMEM),
        scratch_shapes=[VMEM((rows + 8, channels), F32)],
        input_output_aliases={9: 0},
        cost_estimate=pl.CostEstimate(
            flops=4 * layers * rows * channels * hidden,
            bytes_accessed=4 * layers * channels * hidden,
            transcendentals=layers * rows * hidden,
        ),
        compiler_params=pltpu.CompilerParams(vmem_limit_bytes=ROOM),
        name="refine",
    )(
        spots,
        *near(gathered, projected, *params, zeros),
    )
    received = exchange(placed, SECOND)
    return pl.pallas_call(
        blend_kernel,
        out_shape=jax.ShapeDtypeStruct((1, tiles * tile_pos, channels), BF16),
        in_specs=[spec(VMEM)] * 2,
        out_specs=spec(VMEM),
        compiler_params=pltpu.CompilerParams(vmem_limit_bytes=ROOM),
        name="blend",
    )(*near(received, weights))


def solution(mesh):
    in_specs = (
        P(("groups", "frame"), None, None),
        P(("groups", "frame"), None, None, None),
        P("groups"),
        P("groups", None),
        P("groups"),
        P(),
        P(),
        P(),
        P(),
        P(),
        P(),
        P(),
    )
    out_specs = P(("groups", "frame"), None, None)
    return jax.shard_map(
        on_device, mesh=mesh, in_specs=in_specs, out_specs=out_specs, check_vma=False
    )
```

```python
import functools

import jax
import jax.numpy as jnp
from jax import lax
from jax.experimental import pallas as pl
from jax.experimental.pallas import tpu as pltpu
from jax.sharding import PartitionSpec as P

F32 = jnp.float32
BF16 = jnp.bfloat16
VMEM = pltpu.VMEM
SMEM = pltpu.SMEM
ROOM = 24 << 20


def dot(a, b):
    return jnp.dot(a, b, preferred_element_type=F32)


def silu(x):
    half = 0.5 * x
    return half + half * jnp.tanh(half)


def spec(space):
    return pl.BlockSpec(memory_space=space)


def near(*arrays):
    return tuple(pltpu.with_memory_space_constraint(array, VMEM) for array in arrays)


def far(*arrays):
    return tuple(pltpu.with_memory_space_constraint(array, pltpu.HBM) for array in arrays)


FIRST = (11, 10, 9, 8, 3, 2, 1, 0, 7, 6, 5, 4, 15, 14, 13, 12)
SECOND = (11, 10, 4, 8, 13, 6, 15, 0, 7, 1, 5, 12, 9, 3, 2, 14)


def order_of(count, cells):
    width = count // len(cells)
    if width * len(cells) != count:
        return list(range(count))
    return [cell * width + k for cell in cells for k in range(width)]


def ranks_of(count, cells):
    order = order_of(count, cells)
    return [order.index(frame) for frame in range(count)]


def exchange(blocks, cells):
    order = order_of(blocks.shape[0], cells)
    return lax.all_to_all(
        blocks, "frame", split_axis=0, concat_axis=0, tiled=True, axis_index_groups=[order]
    )


def pick_kernel(tiles, assign_ref, low_ref, out_ref):
    count, low_pos, _ = out_ref.shape
    for slot, rank in enumerate(ranks_of(count, FIRST)):
        tile = lax.rem(assign_ref[slot], tiles)
        first = pl.multiple_of(tile * low_pos, low_pos)
        out_ref[rank] = low_ref[0, pl.ds(first, low_pos), :]


def side_kernel(
    tiles, assign_ref, starts_ref, blend_ref, noisy_ref, noise_w_ref, *refs
):
    moved = (len(refs) - 7) // 2
    sources, targets, ranks_ref, sems = refs[:moved], refs[moved + 5 : -2], refs[-2], refs[-1]
    projected_ref, weights_ref, placed_ref, spots_ref, owners_ref = refs[moved : moved + 5]
    copies = [
        pltpu.make_async_copy(source, target, sems.at[k])
        for k, (source, target) in enumerate(zip(sources, targets))
    ]
    for copy in copies:
        copy.start()
    count = assign_ref.shape[0]
    windows, window_len = blend_ref.shape
    channels = noisy_ref.shape[-1]
    tile_pos = noisy_ref.shape[2]
    rows = projected_ref.shape[0]
    own = lax.axis_index("frame")
    projected_ref[...] = dot(noisy_ref[0].reshape(rows, channels), noise_w_ref[...])
    for side, cells in enumerate((FIRST, SECOND)):
        for frame, rank in enumerate(ranks_of(count, cells)):
            ranks_ref[side * count + frame] = rank
    start = starts_ref[assign_ref[own] // tiles]
    for k in range(window_len + 2):
        frame = start + k - 1
        inside = (frame >= 0) & (frame < count)
        near_frame = jnp.clip(frame, 0, count - 1)
        spots_ref[k] = jnp.where(inside, ranks_ref[near_frame], -1)
        spots_ref[window_len + 2 + k] = ranks_ref[count + near_frame]
    placed_ref[...] = jnp.zeros_like(placed_ref)

    def factor_of(window):
        offset = own - starts_ref[window]
        inside = (offset >= 0) & (offset < window_len)
        clipped = jnp.clip(offset, 0, window_len - 1)
        return jnp.where(inside, blend_ref[window, clipped], 0)

    denom = lax.fori_loop(
        0, windows, lambda w, total: total + factor_of(w), jnp.int32(0), unroll=min(windows, 4)
    )
    denom_row = jnp.full((1, channels), denom, jnp.int32).astype(F32)
    for window in range(windows):
        factor_row = jnp.full((1, channels), factor_of(window), jnp.int32).astype(F32)
        weights_ref[window : window + 1, :] = factor_row / denom_row
    for slot in range(count):
        owners_ref[assign_ref[slot]] = ranks_ref[count + slot]
    for copy in copies:
        copy.wait()


def refine_kernel(
    spots_ref, tile_ref, projected_ref, base_w_ref, cond_w_ref, gains_ref, tconv_ref, mlp_in_ref,
    mlp_out_ref, zeros_ref, placed_ref, state_ref,
):
    _, low_pos, channels = tile_ref.shape
    rows = projected_ref.shape[0]
    tile_pos = placed_ref.shape[1]
    window_len = rows // tile_pos
    low_rows = window_len * low_pos

    def low_frame(k):
        spot = spots_ref[k]
        frame = tile_ref[jnp.maximum(spot, 0)]
        if 0 < k <= window_len:
            return frame
        return jnp.where(spot >= 0, frame, jnp.zeros_like(frame))

    frames = [low_frame(k) for k in range(window_len + 2)]
    taps = base_w_ref.shape[0]
    shifted = [jnp.concatenate(frames[k : k + window_len], 0) for k in range(taps)]
    total = dot(
        jnp.concatenate(shifted, 1), base_w_ref[...].reshape(taps * channels, channels)
    )
    base = (shifted[1].astype(F32) + silu(total)).astype(BF16)
    cond = dot(base, cond_w_ref[...])
    ratio = tile_pos // low_pos
    for k in range(ratio):
        state_ref[pl.ds(k, low_rows, stride=ratio), :] = cond
    state = state_ref[:rows] + projected_ref[...]
    for layer in range(gains_ref.shape[0]):
        inverse = lax.rsqrt(jnp.mean(state * state, axis=-1, keepdims=True) + 1e-06)
        scaled = state * inverse
        gain = 0.5 * gains_ref[layer : layer + 1, :]
        previous, same, following = (
            gain * tconv_ref[layer, 0:1, :],
            gain * (1.0 + tconv_ref[layer, 1:2, :]),
            gain * tconv_ref[layer, 2:3, :],
        )
        block = [scaled[k * tile_pos : (k + 1) * tile_pos] for k in range(window_len)]
        parts = []
        for k in range(window_len):
            mixed = same * block[k]
            if k > 0:
                mixed = mixed + previous * block[k - 1]
            if k + 1 < window_len:
                mixed = mixed + following * block[k + 1]
            parts.append(mixed.astype(BF16))
        half = dot(jnp.concatenate(parts, 0), mlp_in_ref[layer])
        hidden = (half + half * jnp.tanh(half)).astype(BF16)
        state = state + dot(hidden, mlp_out_ref[layer])
    refined = state.astype(BF16).reshape(window_len, tile_pos, channels)
    for frame in range(window_len):
        placed_ref[spots_ref[window_len + 3 + frame]] = refined[frame]


def blend_kernel(owners_ref, received_ref, weights_ref, video_ref):
    tile_pos = received_ref.shape[1]
    windows = weights_ref.shape[0]
    tiles = received_ref.shape[0] // windows
    for t in range(tiles):
        total = None
        for window in range(windows):
            block = received_ref[owners_ref[window * tiles + t]].astype(F32)
            term = weights_ref[window : window + 1, :] * block
            total = term if total is None else total + term
        video_ref[0, t * tile_pos : (t + 1) * tile_pos, :] = total.astype(BF16)


def on_device(
    lowres, noisy, starts, blend, assign, base_w, cond_w, noise_w, gains, tconv, mlp_in, mlp_out
):
    count = assign.shape[0]
    windows, window_len = blend.shape
    tiles = count // windows
    tile_pos, channels = noisy.shape[2:]
    low_pos = lowres.shape[1] // tiles
    rows = window_len * tile_pos
    hidden = mlp_in.shape[-1]
    layers = gains.shape[0]

    outgoing = pl.pallas_call(
        functools.partial(pick_kernel, tiles),
        out_shape=VMEM((count, low_pos, channels), BF16),
        in_specs=[spec(SMEM), spec(VMEM)],
        out_specs=spec(VMEM),
        compiler_params=pltpu.CompilerParams(vmem_limit_bytes=ROOM),
        name="pick",
    )(*far(assign, lowres))
    gathered = exchange(outgoing, FIRST)

    moved = (base_w, cond_w, gains, tconv, mlp_in, mlp_out)
    projected, weights, zeros, spots, owners, *params = pl.pallas_call(
        functools.partial(side_kernel, tiles),
        out_shape=(
            VMEM((rows, channels), F32),
            VMEM((windows, channels), F32),
            VMEM((count, tile_pos, channels), BF16),
            SMEM((2 * (window_len + 2),), jnp.int32),
            SMEM((count,), jnp.int32),
            *(VMEM(array.shape, array.dtype) for array in moved),
        ),
        in_specs=[spec(SMEM)] * 3 + [spec(VMEM)] * 2 + [spec(pl.ANY)] * len(moved),
        out_specs=(*(spec(VMEM),) * 3, *(spec(SMEM),) * 2, *(spec(VMEM),) * len(moved)),
        scratch_shapes=[
            SMEM((2 * count,), jnp.int32),
            pltpu.SemaphoreType.DMA((len(moved),)),
        ],
        cost_estimate=pl.CostEstimate(
            flops=2 * rows * channels * channels, bytes_accessed=4 * rows * channels, transcendentals=0
        ),
        compiler_params=pltpu.CompilerParams(vmem_limit_bytes=ROOM),
        name="side",
    )(*far(assign, starts, blend, noisy, noise_w, *moved))

    placed = pl.pallas_call(
        refine_kernel,
        out_shape=VMEM((count, tile_pos, channels), BF16),
        in_specs=[spec(SMEM)] + [spec(VMEM)] * 9,
        out_specs=spec(VMEM),
        scratch_shapes=[VMEM((rows + 8, channels), F32)],
        input_output_aliases={9: 0},
        cost_estimate=pl.CostEstimate(
            flops=4 * layers * rows * channels * hidden,
            bytes_accessed=4 * layers * channels * hidden,
            transcendentals=layers * rows * hidden,
        ),
        compiler_params=pltpu.CompilerParams(vmem_limit_bytes=ROOM),
        name="refine",
    )(
        spots,
        *near(gathered, projected, *params, zeros),
    )
    received = exchange(placed, SECOND)
    return pl.pallas_call(
        blend_kernel,
        out_shape=jax.ShapeDtypeStruct((1, tiles * tile_pos, channels), BF16),
        in_specs=[spec(SMEM)] + [spec(VMEM)] * 2,
        out_specs=spec(VMEM),
        compiler_params=pltpu.CompilerParams(vmem_limit_bytes=ROOM),
        name="blend",
    )(owners, *near(received, weights))


def solution(mesh):
    in_specs = (
        P(("groups", "frame"), None, None),
        P(("groups", "frame"), None, None, None),
        P("groups"),
        P("groups", None),
        P("groups"),
        P(),
        P(),
        P(),
        P(),
        P(),
        P(),
        P(),
    )
    out_specs = P(("groups", "frame"), None, None)
    return jax.shard_map(
        on_device, mesh=mesh, in_specs=in_specs, out_specs=out_specs, check_vma=False
    )
```
